512 devices in a mesh: seq: 64 (over z, y), head: 8 (over x, core).
Axes of the slice: x: 4, y: 8, z: 8, core: 2. Of those that a mesh axis runs over, the one named last changes fastest.
Arguments:
- queries: bfloat16 [32768, 4096], P('seq', 'head'), may hold values from -6 to 6
- keys: bfloat16 [32768, 4096], P('seq', 'head'), may hold values from -6 to 6
- values: bfloat16 [32768, 4096], P('seq', 'head'), may hold values from -6 to 6
- decay_codes: int32 [32], P('head'), may hold values from 4 to 21
- gain: bfloat16 [4096], P('head'), may hold values from 0.099609375 to 1.8984375
- grad_out: bfloat16 [32768, 4096], P('seq', 'head'), may hold values from -6 to 6
Outputs:
- normalized: bfloat16 [32768, 4096], P('seq', 'head')
- grad_queries: bfloat16 [32768, 4096], P('seq', 'head')
- grad_keys: bfloat16 [32768, 4096], P('seq', 'head')
- grad_values: bfloat16 [32768, 4096], P('seq', 'head')
The draws below stay inside these ranges and needn't reach their ends.
All inputs are finite; a program needn't handle non-finite values.
Results may differ from the reference program's by a relative error of at most 0.01015.
Values may be sent and summed in bfloat16 or wider, within the bound.
A program may use at most 128 MiB of HBM per device.

```python
import jax
import jax.numpy as jnp
from jax import lax

HEADS = 32
HEAD_DIM = 128
TOK_DEV = 512
TOKENS = 32768
FEATURES = 4096


def set_ends(drawn, own_key, smallest, top_value):
    dims = drawn.shape
    spot = [jax.random.randint(jax.random.fold_in(own_key, axis), (), 0, dims[axis]) for axis in range(len(dims))]
    drawn = drawn.at[tuple(spot)].set(smallest)
    longest = dims.index(max(dims))
    spot[longest] = (spot[longest] + 1) % dims[longest]
    return drawn.at[tuple(spot)].set(top_value)


def level_of(rng, extent, split, low, top_value):
    factor_of, own = 1.0, jax.random.fold_in(rng, 6)
    for dim, shards_of in split:
        heights = jnp.exp(jax.random.uniform(jax.random.fold_in(own, dim), (shards_of,), jnp.float32, low / len(split), top_value / len(split)))
        factor_of = factor_of * jnp.repeat(heights, extent[dim] // shards_of).reshape([-1 if axis == dim else 1 for axis in range(len(extent))])
    return factor_of


def gaussian(stream_key, shape, deviation, bound, shards=(), held_as=jnp.bfloat16):
    values = deviation * jax.random.normal(stream_key, shape, jnp.float32)
    if shards:
        values = values * level_of(stream_key, shape, shards, -0.22, 0.18)
    return jnp.clip(values, -bound, bound).astype(held_as)


def setup_inputs(seed: int = 0) -> dict:
    arg_keys = jax.random.split(jax.random.key(seed), 7)
    queries = gaussian(arg_keys[0], (TOKENS, FEATURES), 1.0, 6.0, ((0, 64), (1, 8)))
    keys = gaussian(arg_keys[1], (TOKENS, FEATURES), 1.0, 6.0, ((0, 64), (1, 8)))
    values = gaussian(arg_keys[2], (TOKENS, FEATURES), 1.0, 6.0, ((0, 64), (1, 8)))
    decay_codes = set_ends(jax.random.randint(arg_keys[3], (HEADS,), 4, 22), jax.random.fold_in(arg_keys[3], 1), 4, 21).astype(jnp.int32)
    gain = jnp.clip(1.0 + 0.18 * jax.random.normal(arg_keys[4], (FEATURES,), jnp.float32), 0.099609375, 1.8984375).astype(jnp.bfloat16)
    grad_out = gaussian(arg_keys[5], (TOKENS, FEATURES), 1.0, 6.0, ((0, 64), (1, 8)))
    return dict(queries=queries, keys=keys, values=values, decay_codes=decay_codes, gain=gain, grad_out=grad_out)


EPSILON = 1e-06

def rounded(array_in):
    return lax.optimization_barrier(array_in.astype(jnp.bfloat16)).astype(jnp.float32)

def reference(queries, keys, values, decay_codes, gain, grad_out):
    block_count = TOKENS // TOK_DEV
    shape4 = (block_count, TOK_DEV, HEADS, HEAD_DIM)
    query_blocks = queries.reshape(shape4)
    key_blocks = keys.reshape(shape4)
    value_blocks = values.reshape(shape4)
    grad_blocks = grad_out.reshape(shape4)
    log_rates = jnp.log1p(-jnp.exp2(-decay_codes.astype(jnp.float32)))
    positions = jnp.arange(TOK_DEV).astype(jnp.float32)
    offsets = positions[:, None] - positions[None, :]
    decay_mat = jnp.where(offsets[None] >= 0, jnp.exp(jnp.maximum(offsets, 0.0)[None] * log_rates[:, None, None]), 0.0)
    decay_near = jnp.exp(positions[:, None] * log_rates[None, :])[:, :, None]
    decay_after = jnp.exp((positions[:, None] + 1.0) * log_rates[None, :])[:, :, None]
    decay_far = jnp.exp((TOK_DEV - 1.0 - positions)[:, None] * log_rates[None, :])[:, :, None]
    decay_lead = jnp.exp((TOK_DEV - positions)[:, None] * log_rates[None, :])[:, :, None]
    block_pow = jnp.exp(TOK_DEV * log_rates)[:, None, None]
    gain_grid = gain.astype(jnp.float32).reshape(HEADS, HEAD_DIM)

    def forward_block(state, pieces):
        block_query, block_key, block_value, block_grad = pieces
        query_f = block_query.astype(jnp.float32)
        key_f = block_key.astype(jnp.float32)
        value_f = block_value.astype(jnp.float32)
        scores = jnp.einsum('ihd,jhd->hij', query_f, key_f)
        weights = rounded(scores * decay_mat)
        state_bf = rounded(state)
        attended = jnp.einsum('hij,jhd->ihd', weights, value_f)
        attended = attended + decay_near * jnp.einsum('ihd,hde->ihe', query_f, state_bf)
        decayed_keys = rounded(key_f * decay_lead)
        local_state = jnp.einsum('jhd,jhe->hde', decayed_keys, value_f)
        mean_sq = lax.optimization_barrier(jnp.sum(attended * attended, axis=(1, 2))) / FEATURES
        inverse_rms = lax.rsqrt(mean_sq + EPSILON)[:, None, None]
        normalized = (attended * inverse_rms * gain_grid).astype(jnp.bfloat16)
        gained_grad = gain_grid * block_grad.astype(jnp.float32)
        cross_sum = lax.optimization_barrier(jnp.sum(gained_grad * attended, axis=(1, 2)))[:, None, None]
        grad_att = rounded(inverse_rms * gained_grad - inverse_rms * inverse_rms * inverse_rms * cross_sum / FEATURES * attended)
        back_weights = rounded(jnp.einsum('ihe,jhe->hij', grad_att, value_f) * decay_mat)
        grad_query = jnp.einsum('hij,jhd->ihd', back_weights, key_f)
        grad_query = grad_query + decay_near * jnp.einsum('ihe,hde->ihd', grad_att, state_bf)
        key_part = jnp.einsum('hij,ihd->jhd', back_weights, query_f)
        value_part = jnp.einsum('hij,ihe->jhe', weights, grad_att)
        decayed_queries = rounded(query_f * decay_after)
        local_back = jnp.einsum('ihd,ihe->hde', decayed_queries, grad_att)
        new_state = block_pow * state + local_state
        return (new_state, (normalized, grad_query.astype(jnp.bfloat16), key_part, value_part, local_back))
    start = jnp.zeros((HEADS, HEAD_DIM, HEAD_DIM), jnp.float32)
    final_state, results = lax.scan(forward_block, start, (query_blocks, key_blocks, value_blocks, grad_blocks))
    normalized, grad_queries, key_parts, value_parts, local_backs = results

    def backward_block(leaving, pieces):
        local_back, block_key, block_value, key_part, value_part = pieces
        leaving_bf = rounded(leaving)
        grad_key = key_part + decay_far * jnp.einsum('jhe,hde->jhd', block_value.astype(jnp.float32), leaving_bf)
        grad_value = value_part + decay_far * jnp.einsum('jhd,hde->jhe', block_key.astype(jnp.float32), leaving_bf)
        new_leaving = block_pow * leaving + local_back
        return (new_leaving, (grad_key.astype(jnp.bfloat16), grad_value.astype(jnp.bfloat16)))
    final_back, grads = lax.scan(backward_block, start, (local_backs, key_blocks, value_blocks, key_parts, value_parts), reverse=True)
    grad_keys, grad_values = grads
    flat = (TOKENS, FEATURES)
    return (normalized.reshape(flat), grad_queries.reshape(flat), grad_keys.reshape(flat), grad_values.reshape(flat))
```

```python
import functools

import jax
import jax.numpy as jnp
from jax import lax
from jax.experimental import pallas as pl
from jax.experimental.pallas import tpu as pltpu
from jax.sharding import PartitionSpec as P

HEAD_DIM = 128
EPSILON = 1e-06
ROW = 8
HALF = 256
F32 = jnp.float32
BF16 = jnp.bfloat16
MESH = pl.DeviceIdType.MESH


def dot(a, b, ca, cb):
    return lax.dot_general(a, b, (((ca,), (cb,)), ((), ())), preferred_element_type=F32)


def kernel(
    row, planes, peers,
    codes_ref, q_ref, k_ref, v_ref, gain_ref, go_ref,
    norm_ref, gq_ref, gk_ref, gv_ref,
    decay_ref, w_ref, att_ref, gg_ref, ga_ref, dq_ref, acck_ref, accv_ref,
    state_ref, row_recv, pre_ref, tot_ref, plane_recv, full_ref, back_recv,
    part_ref, peer_recv,
    row_send, row_sem, plane_send, plane_sem, back_send, back_sem, peer_send, peer_sem,
):
    tok, width = q_ref.shape
    heads = width // HEAD_DIM
    part_rows = HEAD_DIM // row
    seq = lax.axis_index("seq")
    me = lax.axis_index("head")
    z, y = seq // row, lax.rem(seq, row)

    def row_peer(o):
        return lax.rem(y + o, row)

    barrier = pltpu.get_barrier_semaphore()
    for o in range(1, row):
        pl.semaphore_signal(
            barrier, inc=1, device_id=(z * row + row_peer(o), me), device_id_type=MESH
        )
    for o in range(1, planes):
        pl.semaphore_signal(
            barrier, inc=1, device_id=(lax.rem(z + o, planes) * row + y, me), device_id_type=MESH
        )
    for o in range(1, peers):
        pl.semaphore_signal(
            barrier, inc=1, device_id=(seq, lax.rem(me + o, peers)), device_id_type=MESH
        )

    def lanes(h):
        return slice(h * HEAD_DIM, (h + 1) * HEAD_DIM)

    rates = []
    for h in range(heads):
        code = jnp.full((8, HALF), codes_ref[h], jnp.int32).astype(F32)
        rates.append(jnp.log1p(-jnp.exp2(-code)))

    positions = lax.broadcasted_iota(jnp.int32, (tok, HEAD_DIM), 0).astype(F32)

    def powers(h, exponent):
        return jnp.exp(exponent * rates[h][0:1, :HEAD_DIM])

    def power(h, n):
        return jnp.exp(F32(n) * rates[h][0:1, :HEAD_DIM])

    def row_copy(s, o):
        return pltpu.make_async_remote_copy(
            src_ref=state_ref.at[s, row_peer(o)],
            dst_ref=row_recv.at[s, y],
            send_sem=row_send.at[s, o],
            recv_sem=row_sem.at[s, o],
            device_id=(z * row + row_peer(o), me),
            device_id_type=MESH,
        )

    def plane_copy(s, o):
        to = z + o if s == 0 else z - o
        return pltpu.make_async_remote_copy(
            src_ref=tot_ref.at[s],
            dst_ref=plane_recv.at[s, z],
            send_sem=plane_send.at[s, o],
            recv_sem=plane_sem.at[s, o],
            device_id=(lax.rem(to + planes, planes) * row + y, me),
            device_id_type=MESH,
        )

    def back_copy(s, o):
        return pltpu.make_async_remote_copy(
            src_ref=full_ref.at[s, row_peer(o)],
            dst_ref=back_recv.at[s, y],
            send_sem=back_send.at[s, o],
            recv_sem=back_sem.at[s, o],
            device_id=(z * row + row_peer(o), me),
            device_id_type=MESH,
        )

    def sends_plane(s, o):
        return z + o < planes if s == 0 else z - o >= 0

    def takes_plane(s, o):
        return z - o >= 0 if s == 0 else z + o < planes

    def put_state(s, h, value):
        state_ref[s, :, h] = value.astype(BF16).reshape(row, part_rows, HEAD_DIM)

    def start_row(s):
        for o in range(1, row):
            row_copy(s, o).start()
        row_recv[s, y] = state_ref[s, y]

    def turn_row(s):
        for o in range(1, row):
            row_copy(s, o).wait_recv()
        for h in range(heads):
            step = power(h, tok)
            held = jnp.zeros((part_rows, HEAD_DIM), F32)
            for c in range(row) if s == 0 else reversed(range(row)):
                pre_ref[s, c, h] = held
                held = step * held + row_recv[s, c, h].astype(F32)
            tot_ref[s, h] = held.astype(BF16)
        for o in range(1, planes):
            @pl.when(sends_plane(s, o))
            def _():
                plane_copy(s, o).start()

    def turn_plane(s):
        for o in range(1, planes):
            @pl.when(takes_plane(s, o))
            def _():
                plane_copy(s, o).wait_recv()
        zero = tuple(jnp.zeros((part_rows, HEAD_DIM), F32) for _ in range(heads))
        leap = [power(h, tok * row) for h in range(heads)]

        def add(t, held):
            at = t if s == 0 else planes - 1 - t
            return tuple(
                leap[h] * held[h] + plane_recv[s, at, h].astype(F32) for h in range(heads)
            )

        held = lax.fori_loop(0, z if s == 0 else planes - 1 - z, add, zero)
        for h in range(heads):
            for c in range(row):
                far = c if s == 0 else row - 1 - c
                full_ref[s, c, h] = (pre_ref[s, c, h] + power(h, tok * far) * held[h]).astype(BF16)
        for o in range(1, row):
            back_copy(s, o).start()
        back_recv[s, y] = full_ref[s, y]

    def end_scan(s):
        for o in range(1, row):
            back_copy(s, o).wait_recv()

    def crossing(s, h):
        return back_recv[s, :, h].reshape(HEAD_DIM, HEAD_DIM)

    for h in range(heads):
        lead = powers(h, F32(tok) - positions)
        decayed = (k_ref[:, lanes(h)].astype(F32) * lead).astype(BF16)
        put_state(0, h, dot(decayed, v_ref[:, lanes(h)], 0, 0))

    pl.semaphore_wait(barrier, row + planes + peers - 3)
    start_row(0)

    halves = tok // HALF
    blocks = [(r, c) for r in range(halves) for c in range(r + 1)]

    def rows_of(r):
        return slice(r * HALF, (r + 1) * HALF)

    def local_forward(h):
        at = lanes(h)
        offset = (
            lax.broadcasted_iota(jnp.int32, (HALF, HALF), 0)
            - lax.broadcasted_iota(jnp.int32, (HALF, HALF), 1)
        ).astype(F32)
        rate = rates[h][0:1, :]
        for d in range(halves):
            away = offset + F32(d * HALF)
            value = jnp.exp(jnp.maximum(away, 0.0) * rate)
            if d == 0:
                value = jnp.where(away >= 0, value, 0.0)
            decay_ref[h, d] = value
        for r in range(halves):
            total = None
            for c in range(r + 1):
                scores = dot(q_ref[rows_of(r), at], k_ref[rows_of(c), at], 1, 1)
                weights = (scores * decay_ref[h, r - c]).astype(BF16)
                w_ref[h, blocks.index((r, c))] = weights
                term = dot(weights, v_ref[rows_of(c), at], 1, 0)
                total = term if total is None else total + term
            att_ref[rows_of(r), at] = total
        after = powers(h, positions + 1.0)
        dq_ref[:, at] = (q_ref[:, at].astype(F32) * after).astype(BF16)
        gg_ref[:, at] = gain_ref[0:1, at].astype(F32) * go_ref[:, at].astype(F32)

    local_forward(0)
    local_forward(1)
    turn_row(0)
    local_forward(2)
    turn_plane(0)
    local_forward(3)
    end_scan(0)

    squares = jnp.zeros((tok, HEAD_DIM), F32)
    crosses = jnp.zeros((tok, HEAD_DIM), F32)
    for h in range(heads):
        at = lanes(h)
        near = powers(h, positions)
        att = att_ref[:, at] + near * dot(q_ref[:, at], crossing(0, h), 1, 0)
        att_ref[:, at] = att
        squares = squares + att * att
        crosses = crosses + gg_ref[:, at] * att
    part_ref[0:1, :] = jnp.sum(squares.T, axis=0, keepdims=True)
    part_ref[1:2, :] = jnp.sum(crosses.T, axis=0, keepdims=True)

    def peer_copy(o):
        return pltpu.make_async_remote_copy(
            src_ref=part_ref,
            dst_ref=peer_recv.at[me],
            send_sem=peer_send.at[o],
            recv_sem=peer_sem.at[o],
            device_id=(seq, lax.rem(me + o, peers)),
            device_id_type=MESH,
        )

    for o in range(1, peers):
        peer_copy(o).start()
    peer_recv[me] = part_ref[...]
    for o in range(1, peers):
        peer_copy(o).wait_recv()
    sums = peer_recv[0]
    for p in range(1, peers):
        sums = sums + peer_recv[p]
    features = F32(width * peers)
    inverse_row = lax.rsqrt(sums[0:1, :] / features + EPSILON)
    mean_row = inverse_row * sums[1:2, :] / features
    inverse = jnp.broadcast_to(inverse_row, (HEAD_DIM, tok)).T
    mean = jnp.broadcast_to(mean_row, (HEAD_DIM, tok)).T

    for h in range(heads):
        at = lanes(h)
        unit = att_ref[:, at] * inverse
        norm_ref[:, at] = (unit * gain_ref[0:1, at].astype(F32)).astype(BF16)
        grad = (inverse * (gg_ref[:, at] - unit * mean)).astype(BF16)
        ga_ref[:, at] = grad
        put_state(1, h, dot(dq_ref[:, at], grad, 0, 0))
    start_row(1)

    def local_backward(h):
        at = lanes(h)
        to_q = [None] * halves
        to_k = [None] * halves
        to_v = [None] * halves

        def add(old, new):
            return new if old is None else old + new

        for r, c in blocks:
            grad = ga_ref[rows_of(r), at]
            back = dot(grad, v_ref[rows_of(c), at], 1, 1)
            back = (back * decay_ref[h, r - c]).astype(BF16)
            to_q[r] = add(to_q[r], dot(back, k_ref[rows_of(c), at], 1, 0))
            to_k[c] = add(to_k[c], dot(back, q_ref[rows_of(r), at], 0, 0))
            to_v[c] = add(to_v[c], dot(w_ref[h, blocks.index((r, c))], grad, 0, 0))
        for r in range(halves):
            near = powers(h, positions[rows_of(r), :])
            grad = ga_ref[rows_of(r), at]
            gq_ref[rows_of(r), at] = (
                to_q[r] + near * dot(grad, crossing(0, h), 1, 1)
            ).astype(BF16)
            acck_ref[rows_of(r), at] = to_k[r]
            accv_ref[rows_of(r), at] = to_v[r]

    local_backward(0)
    local_backward(1)
    turn_row(1)
    local_backward(2)
    turn_plane(1)
    local_backward(3)
    end_scan(1)

    for h in range(heads):
        at = lanes(h)
        far = powers(h, F32(tok - 1) - positions)
        left = crossing(1, h)
        gk_ref[:, at] = (acck_ref[:, at] + far * dot(v_ref[:, at], left, 1, 1)).astype(BF16)
        gv_ref[:, at] = (accv_ref[:, at] + far * dot(k_ref[:, at], left, 1, 0)).astype(BF16)

    for s in range(2):
        for o in range(1, row):
            row_copy(s, o).wait_send()
            back_copy(s, o).wait_send()
        for o in range(1, planes):
            @pl.when(sends_plane(s, o))
            def _():
                plane_copy(s, o).wait_send()
    for o in range(1, peers):
        peer_copy(o).wait_send()


def body(row, planes, peers, queries, keys, values, decay_codes, gain, grad_out):
    tok, width = queries.shape
    heads = width // HEAD_DIM
    part_rows = HEAD_DIM // row
    halves = tok // HALF
    slices = (heads, part_rows, HEAD_DIM)
    vmem = pl.BlockSpec(memory_space=pltpu.VMEM)
    out = jax.ShapeDtypeStruct((tok, width), BF16)
    wide = pltpu.VMEM((tok, width), F32)
    thin = pltpu.VMEM((tok, width), BF16)
    return pl.pallas_call(
        functools.partial(kernel, row, planes, peers),
        out_shape=(out,) * 4,
        in_specs=[pl.BlockSpec(memory_space=pltpu.SMEM)] + [vmem] * 5,
        out_specs=(vmem,) * 4,
        scratch_shapes=[
            pltpu.VMEM((heads, halves, HALF, HALF), F32),
            pltpu.VMEM((heads, halves * (halves + 1) // 2, HALF, HALF), BF16),
            wide, wide, thin, thin, wide, wide,
            pltpu.VMEM((2, row) + slices, BF16),
            pltpu.VMEM((2, row) + slices, BF16),
            pltpu.VMEM((2, row) + slices, F32),
            pltpu.VMEM((2,) + slices, BF16),
            pltpu.VMEM((2, planes) + slices, BF16),
            pltpu.VMEM((2, row) + slices, BF16),
            pltpu.VMEM((2, row) + slices, BF16),
            pltpu.VMEM((2, tok), F32),
            pltpu.VMEM((peers, 2, tok), F32),
            pltpu.SemaphoreType.DMA((2, row)),
            pltpu.SemaphoreType.DMA((2, row)),
            pltpu.SemaphoreType.DMA((2, planes)),
            pltpu.SemaphoreType.DMA((2, planes)),
            pltpu.SemaphoreType.DMA((2, row)),
            pltpu.SemaphoreType.DMA((2, row)),
            pltpu.SemaphoreType.DMA((peers,)),
            pltpu.SemaphoreType.DMA((peers,)),
        ],
        compiler_params=pltpu.CompilerParams(
            collective_id=0, has_side_effects=True, vmem_limit_bytes=56 * 1024 * 1024
        ),
        name="lightning",
    )(decay_codes, queries, keys, values, gain.reshape(1, width), grad_out)


def solution(mesh):
    split = P("seq", "head")
    planes = mesh.shape["seq"] // ROW
    return jax.shard_map(
        functools.partial(body, ROW, planes, mesh.shape["head"]),
        mesh=mesh,
        in_specs=(split, split, split, P("head"), P("head"), split),
        out_specs=(split,) * 4,
        check_vma=False,
    )
```

```python
import functools

import jax
import jax.numpy as jnp
from jax import lax
from jax.experimental import pallas as pl
from jax.experimental.pallas import tpu as pltpu
from jax.sharding import PartitionSpec as P

HEAD_DIM = 128
EPSILON = 1e-06
ROW = 8
HALF = 256
GROUPS = 2
VMEM_A = 67043328
VMEM_B = 67043328
F32 = jnp.float32
BF16 = jnp.bfloat16
MESH = pl.DeviceIdType.MESH


def dot(a, b, ca, cb):
    return lax.dot_general(a, b, (((ca,), (cb,)), ((), ())), preferred_element_type=F32)


def kernel(
    row, planes, peers,
    codes_hbm, q_hbm, k_hbm, v_hbm, gain_hbm, go_hbm,
    norm_out, gq_out, acck_out, accv_out, left_ref,
    codes_ref, gain_ref, q_ref, k_ref, v_ref, go_ref, norm_ref, gq_ref, acck_ref, accv_ref,
    decay_ref, w_ref, att_ref, gg_ref, ga_ref, dq_ref, near_ref,
    state_ref, row_recv, pre_ref, tot_ref, plane_recv, full_ref, back_recv,
    part_ref, peer_recv, load_sem, store_sem,
    row_send, row_sem, plane_send, plane_sem, back_send, back_sem, peer_send, peer_sem,
):
    tok, width = q_ref.shape
    heads = width // HEAD_DIM
    part_rows = HEAD_DIM // row
    team = heads // GROUPS
    seq = lax.axis_index("seq")
    me = lax.axis_index("head")
    z, y = seq // row, lax.rem(seq, row)

    def row_peer(o):
        return lax.rem(y + o, row)

    sources = (
        (codes_hbm, codes_ref), (k_hbm, k_ref), (v_hbm, v_ref),
        (q_hbm, q_ref), (gain_hbm, gain_ref), (go_hbm, go_ref),
    )
    results = ((norm_ref, norm_out), (gq_ref, gq_out), (acck_ref, acck_out), (accv_ref, accv_out))

    def load(n):
        return pltpu.make_async_copy(*sources[n], load_sem.at[n])

    def store(n):
        return pltpu.make_async_copy(*results[n], store_sem.at[n])

    for n in range(6):
        load(n).start()

    barrier = pltpu.get_barrier_semaphore()
    for o in range(1, row):
        pl.semaphore_signal(
            barrier, inc=1, device_id=(z * row + row_peer(o), me), device_id_type=MESH
        )
    for o in range(1, planes):
        pl.semaphore_signal(
            barrier, inc=1, device_id=(lax.rem(z + o, planes) * row + y, me), device_id_type=MESH
        )
    for o in range(1, peers):
        pl.semaphore_signal(
            barrier, inc=1, device_id=(seq, lax.rem(me + o, peers)), device_id_type=MESH
        )

    def lanes(h):
        return slice(h * HEAD_DIM, (h + 1) * HEAD_DIM)

    load(0).wait()
    rates = []
    for h in range(heads):
        code = jnp.full((8, HALF), codes_ref[h], jnp.int32).astype(F32)
        rates.append(jnp.log1p(-jnp.exp2(-code)))

    positions = lax.broadcasted_iota(jnp.int32, (tok, HEAD_DIM), 0).astype(F32)

    def powers(h, exponent):
        return jnp.exp(exponent * rates[h][0:1, :HEAD_DIM])

    def power(h, n):
        return jnp.exp(F32(n) * rates[h][0:1, :HEAD_DIM])

    def row_copy(s, g, o):
        return pltpu.make_async_remote_copy(
            src_ref=state_ref.at[s, g, row_peer(o)],
            dst_ref=row_recv.at[s, g, y],
            send_sem=row_send.at[s * GROUPS + g, o],
            recv_sem=row_sem.at[s * GROUPS + g, o],
            device_id=(z * row + row_peer(o), me),
            device_id_type=MESH,
        )

    def plane_copy(s, g, o):
        to = z + o if s == 0 else z - o
        return pltpu.make_async_remote_copy(
            src_ref=tot_ref.at[s, g],
            dst_ref=plane_recv.at[s, g, z],
            send_sem=plane_send.at[s * GROUPS + g, o],
            recv_sem=plane_sem.at[s * GROUPS + g, o],
            device_id=(lax.rem(to + planes, planes) * row + y, me),
            device_id_type=MESH,
        )

    def back_copy(s, g, o):
        return pltpu.make_async_remote_copy(
            src_ref=full_ref.at[s, g, row_peer(o)],
            dst_ref=back_recv.at[s, g, y],
            send_sem=back_send.at[s * GROUPS + g, o],
            recv_sem=back_sem.at[s * GROUPS + g, o],
            device_id=(z * row + row_peer(o), me),
            device_id_type=MESH,
        )

    def sends_plane(s, o):
        return z + o < planes if s == 0 else z - o >= 0

    def takes_plane(s, o):
        return z - o >= 0 if s == 0 else z + o < planes

    def put_state(s, h, value):
        g, t = divmod(h, team)
        state_ref[s, g, :, t] = value.astype(BF16).reshape(row, part_rows, HEAD_DIM)

    def start_row(s, g):
        for o in range(1, row):
            row_copy(s, g, o).start()
        row_recv[s, g, y] = state_ref[s, g, y]

    def turn_row(s, g):
        for o in range(1, row):
            row_copy(s, g, o).wait_recv()
        for t in range(team):
            step = power(g * team + t, tok)
            held = jnp.zeros((part_rows, HEAD_DIM), F32)
            for c in range(row) if s == 0 else reversed(range(row)):
                pre_ref[s, g, c, t] = held
                held = step * held + row_recv[s, g, c, t].astype(F32)
            tot_ref[s, g, t] = held.astype(BF16)
        for o in range(1, planes):
            @pl.when(sends_plane(s, o))
            def _():
                plane_copy(s, g, o).start()

    def turn_plane(s, g):
        for o in range(1, planes):
            @pl.when(takes_plane(s, o))
            def _():
                plane_copy(s, g, o).wait_recv()
        zero = tuple(jnp.zeros((part_rows, HEAD_DIM), F32) for _ in range(team))
        leap = [power(g * team + t, tok * row) for t in range(team)]

        def add(n, held):
            at = n if s == 0 else planes - 1 - n
            return tuple(
                leap[t] * held[t] + plane_recv[s, g, at, t].astype(F32) for t in range(team)
            )

        held = lax.fori_loop(0, z if s == 0 else planes - 1 - z, add, zero)
        for t in range(team):
            for c in range(row):
                far = power(g * team + t, tok * (c if s == 0 else row - 1 - c))
                full_ref[s, g, c, t] = (pre_ref[s, g, c, t] + far * held[t]).astype(BF16)
        for o in range(1, row):
            back_copy(s, g, o).start()
        back_recv[s, g, y] = full_ref[s, g, y]

    def end_scan(s, g):
        for o in range(1, row):
            back_copy(s, g, o).wait_recv()

    def crossing(s, h):
        g, t = divmod(h, team)
        return back_recv[s, g, :, t].reshape(HEAD_DIM, HEAD_DIM)

    leads = [powers(h, F32(tok) - positions) for h in range(heads)]
    load(1).wait()
    load(2).wait()
    for g in range(GROUPS):
        for h in range(g * team, (g + 1) * team):
            decayed = (k_ref[:, lanes(h)].astype(F32) * leads[h]).astype(BF16)
            put_state(0, h, dot(decayed, v_ref[:, lanes(h)], 0, 0))
        if g == 0:
            pl.semaphore_wait(barrier, row + planes + peers - 3)
        start_row(0, g)
    for n in range(3, 6):
        load(n).wait()
    gain = gain_ref[...].astype(F32).reshape(1, width)

    halves = tok // HALF
    blocks = [(r, c) for r in range(halves) for c in range(r + 1)]

    def rows_of(r):
        return slice(r * HALF, (r + 1) * HALF)

    def local_forward(h):
        at = lanes(h)
        offset = (
            lax.broadcasted_iota(jnp.int32, (HALF, HALF), 0)
            - lax.broadcasted_iota(jnp.int32, (HALF, HALF), 1)
        ).astype(F32)
        rate = rates[h][0:1, :]
        for d in range(halves):
            away = offset + F32(d * HALF)
            value = jnp.exp(jnp.maximum(away, 0.0) * rate)
            if d == 0:
                value = jnp.where(away >= 0, value, 0.0)
            decay_ref[h, d] = value
        for r in range(halves):
            total = None
            for c in range(r + 1):
                scores = dot(q_ref[rows_of(r), at], k_ref[rows_of(c), at], 1, 1)
                weights = (scores * decay_ref[h, r - c]).astype(BF16)
                w_ref[h, blocks.index((r, c))] = weights
                term = dot(weights, v_ref[rows_of(c), at], 1, 0)
                total = term if total is None else total + term
            att_ref[rows_of(r), at] = total
        after = powers(h, positions + 1.0)
        dq_ref[:, at] = (q_ref[:, at].astype(F32) * after).astype(BF16)
        near_ref[:, at] = powers(h, positions)
        gg_ref[:, at] = gain[:, at] * go_ref[:, at].astype(F32)

    third = (heads + 1) // 2

    def scan(s, local):
        for h in range(third):
            local(h)
        for g in range(GROUPS):
            turn_row(s, g)
        for h in range(third, (third + heads) // 2):
            local(h)
        for g in range(GROUPS):
            turn_plane(s, g)
        for h in range((third + heads) // 2, heads):
            local(h)

    scan(0, local_forward)

    squares = jnp.zeros((tok, HEAD_DIM), F32)
    crosses = jnp.zeros((tok, HEAD_DIM), F32)
    for h in range(heads):
        at = lanes(h)
        if h % team == 0:
            end_scan(0, h // team)
        att = att_ref[:, at] + near_ref[:, at] * dot(q_ref[:, at], crossing(0, h), 1, 0)
        att_ref[:, at] = att
        squares = squares + att * att
        crosses = crosses + gg_ref[:, at] * att
    part_ref[0:1, :] = jnp.sum(squares.T, axis=0, keepdims=True)
    part_ref[1:2, :] = jnp.sum(crosses.T, axis=0, keepdims=True)

    def peer_copy(o):
        return pltpu.make_async_remote_copy(
            src_ref=part_ref,
            dst_ref=peer_recv.at[me],
            send_sem=peer_send.at[o],
            recv_sem=peer_sem.at[o],
            device_id=(seq, lax.rem(me + o, peers)),
            device_id_type=MESH,
        )

    for o in range(1, peers):
        peer_copy(o).start()
    peer_recv[me] = part_ref[...]
    for o in range(1, peers):
        peer_copy(o).wait_recv()
    sums = peer_recv[0]
    for p in range(1, peers):
        sums = sums + peer_recv[p]
    features = F32(width * peers)
    inverse_row = lax.rsqrt(sums[0:1, :] / features + EPSILON)
    mean_row = inverse_row * sums[1:2, :] / features
    inverse = jnp.broadcast_to(inverse_row, (HEAD_DIM, tok)).T
    mean = jnp.broadcast_to(mean_row, (HEAD_DIM, tok)).T

    for h in range(heads):
        at = lanes(h)
        unit = att_ref[:, at] * inverse
        grad = (inverse * (gg_ref[:, at] - unit * mean)).astype(BF16)
        ga_ref[:, at] = grad
        put_state(1, h, dot(dq_ref[:, at], grad, 0, 0))
        if h % team == team - 1:
            start_row(1, h // team)
    for h in range(heads):
        at = lanes(h)
        norm_ref[:, at] = (att_ref[:, at] * inverse * gain[:, at]).astype(BF16)
    store(0).start()

    def local_backward(h):
        at = lanes(h)
        to_q = [None] * halves
        to_k = [None] * halves
        to_v = [None] * halves

        def add(old, new):
            return new if old is None else old + new

        for r, c in blocks:
            grad = ga_ref[rows_of(r), at]
            back = dot(grad, v_ref[rows_of(c), at], 1, 1)
            back = (back * decay_ref[h, r - c]).astype(BF16)
            to_q[r] = add(to_q[r], dot(back, k_ref[rows_of(c), at], 1, 0))
            to_k[c] = add(to_k[c], dot(back, q_ref[rows_of(r), at], 0, 0))
            to_v[c] = add(to_v[c], dot(w_ref[h, blocks.index((r, c))], grad, 0, 0))
        for r in range(halves):
            near = near_ref[rows_of(r), at]
            grad = ga_ref[rows_of(r), at]
            gq_ref[rows_of(r), at] = (
                to_q[r] + near * dot(grad, crossing(0, h), 1, 1)
            ).astype(BF16)
            acck_ref[rows_of(r), at] = to_k[r].astype(BF16)
            accv_ref[rows_of(r), at] = to_v[r].astype(BF16)

    scan(1, local_backward)
    for n in range(1, 4):
        store(n).start()
    for g in range(GROUPS):
        end_scan(1, g)
        for t in range(team):
            left_ref[g * team + t] = crossing(1, g * team + t)

    for s in range(2):
        for g in range(GROUPS):
            for o in range(1, row):
                row_copy(s, g, o).wait_send()
                back_copy(s, g, o).wait_send()
            for o in range(1, planes):
                @pl.when(sends_plane(s, o))
                def _():
                    plane_copy(s, g, o).wait_send()
    for o in range(1, peers):
        peer_copy(o).wait_send()
    for n in range(4):
        store(n).wait()


def finish(codes_ref, k_ref, v_ref, left_ref, norm_in, gq_in, acck_ref, accv_ref,
           norm_ref, gq_ref, gk_ref, gv_ref):
    tok = k_ref.shape[0]
    code = jnp.full((8, HEAD_DIM), codes_ref[pl.program_id(0)], jnp.int32).astype(F32)
    rate = jnp.log1p(-jnp.exp2(-code))[0:1, :]
    positions = lax.broadcasted_iota(jnp.int32, (tok, HEAD_DIM), 0).astype(F32)
    far = jnp.exp((F32(tok - 1) - positions) * rate)
    left = left_ref[0]
    norm_ref[...] = norm_in[...]
    gq_ref[...] = gq_in[...]
    gk_ref[...] = (acck_ref[...].astype(F32) + far * dot(v_ref[...], left, 1, 1)).astype(BF16)
    gv_ref[...] = (accv_ref[...].astype(F32) + far * dot(k_ref[...], left, 1, 0)).astype(BF16)


def body(row, planes, peers, queries, keys, values, decay_codes, gain, grad_out):
    tok, width = queries.shape
    heads = width // HEAD_DIM
    part_rows = HEAD_DIM // row
    halves = tok // HALF
    team = heads // GROUPS
    slices = (team, part_rows, HEAD_DIM)
    smem = pl.BlockSpec(memory_space=pltpu.SMEM)
    vmem = pl.BlockSpec(memory_space=pltpu.VMEM)
    hbm = pl.BlockSpec(memory_space=pl.ANY)
    far = pl.BlockSpec(memory_space=pltpu.HBM)
    out = jax.ShapeDtypeStruct((tok, width), BF16)
    states = jax.ShapeDtypeStruct((heads, HEAD_DIM, HEAD_DIM), BF16)
    wide = pltpu.VMEM((tok, width), F32)
    thin = pltpu.VMEM((tok, width), BF16)
    dma = pltpu.SemaphoreType.DMA
    normalized, grad_query, key_part, value_part, left = pl.pallas_call(
        functools.partial(kernel, row, planes, peers),
        out_shape=(out,) * 4 + (states,),
        in_specs=[far] * 6,
        out_specs=(hbm,) * 4 + (vmem,),
        scratch_shapes=[pltpu.SMEM((heads,), jnp.int32), pltpu.VMEM((width,), BF16)] + [thin] * 8 + [
            pltpu.VMEM((heads, halves, HALF, HALF), F32),
            pltpu.VMEM((heads, halves * (halves + 1) // 2, HALF, HALF), BF16),
            wide, wide, thin, thin, wide,
            pltpu.VMEM((2, GROUPS, row) + slices, BF16),
            pltpu.VMEM((2, GROUPS, row) + slices, BF16),
            pltpu.VMEM((2, GROUPS, row) + slices, F32),
            pltpu.VMEM((2, GROUPS) + slices, BF16),
            pltpu.VMEM((2, GROUPS, planes) + slices, BF16),
            pltpu.VMEM((2, GROUPS, row) + slices, BF16),
            pltpu.VMEM((2, GROUPS, row) + slices, BF16),
            pltpu.VMEM((2, tok), F32),
            pltpu.VMEM((peers, 2, tok), F32),
            dma((6,)),
            dma((4,)),
            dma((2 * GROUPS, row)),
            dma((2 * GROUPS, row)),
            dma((2 * GROUPS, planes)),
            dma((2 * GROUPS, planes)),
            dma((2 * GROUPS, row)),
            dma((2 * GROUPS, row)),
            dma((peers,)),
            dma((peers,)),
        ],
        compiler_params=pltpu.CompilerParams(
            collective_id=0, has_side_effects=True, vmem_limit_bytes=VMEM_A
        ),
        name="lightning",
    )(decay_codes, queries, keys, values, gain, grad_out)
    column = pl.BlockSpec((tok, HEAD_DIM), lambda h: (0, h))
    return pl.pallas_call(
        finish,
        grid=(heads,),
        out_shape=(out,) * 4,
        in_specs=[smem, column, column, pl.BlockSpec((1, HEAD_DIM, HEAD_DIM), lambda h: (h, 0, 0))]
        + [column] * 4,
        out_specs=(column,) * 4,
        compiler_params=pltpu.CompilerParams(vmem_limit_bytes=VMEM_B),
        name="finish",
    )(decay_codes, keys, values, left, normalized, grad_query, key_part, value_part)


def solution(mesh):
    split = P("seq", "head")
    planes = mesh.shape["seq"] // ROW
    return jax.shard_map(
        functools.partial(body, ROW, planes, mesh.shape["head"]),
        mesh=mesh,
        in_specs=(split, split, split, P("head"), P("head"), split),
        out_specs=(split,) * 4,
        check_vma=False,
    )
```

```python
import functools

import jax
import jax.numpy as jnp
from jax import lax
from jax.experimental import pallas as pl
from jax.experimental.pallas import tpu as pltpu
from jax.sharding import PartitionSpec as P

HEAD_DIM = 128
EPSILON = 1e-06
ROW = 8
HALF = 256
GROUPS = 2
VMEM_A = 62600000
VMEM_B = 16777216
F32 = jnp.float32
BF16 = jnp.bfloat16
MESH = pl.DeviceIdType.MESH


def dot(a, b, ca, cb):
    return lax.dot_general(a, b, (((ca,), (cb,)), ((), ())), preferred_element_type=F32)


def kernel(
    row, planes, peers,
    codes_hbm, q_hbm, k_hbm, v_hbm, gain_hbm, go_hbm,
    norm_ref, gq_ref, acck_ref, accv_ref, left_ref, k_ref, v_ref, far_ref,
    codes_ref, gain_ref, q_ref, go_ref,
    decay_ref, w_ref, att_ref, gg_ref, ga_ref, dq_ref, near_ref,
    state_ref, row_recv, pre_ref, tot_ref, plane_recv, full_ref, back_recv,
    part_ref, peer_recv, load_sem,
    row_send, row_sem, plane_send, plane_sem, back_send, back_sem, peer_send, peer_sem,
):
    tok, width = q_ref.shape
    heads = width // HEAD_DIM
    part_rows = HEAD_DIM // row
    team = heads // GROUPS
    seq = lax.axis_index("seq")
    me = lax.axis_index("head")
    z, y = seq // row, lax.rem(seq, row)

    def row_peer(o):
        return lax.rem(y + o, row)

    sources = (
        (codes_hbm, codes_ref), (k_hbm, k_ref), (v_hbm, v_ref),
        (q_hbm, q_ref), (gain_hbm, gain_ref), (go_hbm, go_ref),
    )

    def load(n):
        return pltpu.make_async_copy(*sources[n], load_sem.at[n])

    for n in range(6):
        load(n).start()

    barrier = pltpu.get_barrier_semaphore()
    for o in range(1, row):
        pl.semaphore_signal(
            barrier, inc=1, device_id=(z * row + row_peer(o), me), device_id_type=MESH
        )
    for o in range(1, planes):
        pl.semaphore_signal(
            barrier, inc=1, device_id=(lax.rem(z + o, planes) * row + y, me), device_id_type=MESH
        )
    for o in range(1, peers):
        pl.semaphore_signal(
            barrier, inc=1, device_id=(seq, lax.rem(me + o, peers)), device_id_type=MESH
        )

    def lanes(h):
        return slice(h * HEAD_DIM, (h + 1) * HEAD_DIM)

    load(0).wait()
    rates = []
    for h in range(heads):
        code = jnp.full((8, HALF), codes_ref[h], jnp.int32).astype(F32)
        rates.append(jnp.log1p(-jnp.exp2(-code)))

    positions = lax.broadcasted_iota(jnp.int32, (tok, HEAD_DIM), 0).astype(F32)

    def powers(h, exponent):
        return jnp.exp(exponent * rates[h][0:1, :HEAD_DIM])

    def power(h, n):
        return jnp.exp(F32(n) * rates[h][0:1, :HEAD_DIM])

    def row_copy(s, g, o):
        return pltpu.make_async_remote_copy(
            src_ref=state_ref.at[s, g, row_peer(o)],
            dst_ref=row_recv.at[s, g, y],
            send_sem=row_send.at[s * GROUPS + g, o],
            recv_sem=row_sem.at[s * GROUPS + g, o],
            device_id=(z * row + row_peer(o), me),
            device_id_type=MESH,
        )

    def plane_copy(s, g, o):
        to = z + o if s == 0 else z - o
        return pltpu.make_async_remote_copy(
            src_ref=tot_ref.at[s, g],
            dst_ref=plane_recv.at[s, g, z],
            send_sem=plane_send.at[s * GROUPS + g, o],
            recv_sem=plane_sem.at[s * GROUPS + g, o],
            device_id=(lax.rem(to + planes, planes) * row + y, me),
            device_id_type=MESH,
        )

    def back_copy(s, g, o):
        return pltpu.make_async_remote_copy(
            src_ref=full_ref.at[s, g, row_peer(o)],
            dst_ref=back_recv.at[s, g, y],
            send_sem=back_send.at[s * GROUPS + g, o],
            recv_sem=back_sem.at[s * GROUPS + g, o],
            device_id=(z * row + row_peer(o), me),
            device_id_type=MESH,
        )

    def sends_plane(s, o):
        return z + o < planes if s == 0 else z - o >= 0

    def takes_plane(s, o):
        return z - o >= 0 if s == 0 else z + o < planes

    def put_state(s, h, value):
        g, t = divmod(h, team)
        state_ref[s, g, :, t] = value.astype(BF16).reshape(row, part_rows, HEAD_DIM)

    def start_row(s, g):
        for o in range(1, row):
            row_copy(s, g, o).start()
        row_recv[s, g, y] = state_ref[s, g, y]

    def turn_row(s, g):
        for o in range(1, row):
            row_copy(s, g, o).wait_recv()
        for t in range(team):
            step = power(g * team + t, tok)
            held = jnp.zeros((part_rows, HEAD_DIM), F32)
            for c in range(row) if s == 0 else reversed(range(row)):
                pre_ref[s, g, c, t] = held
                held = step * held + row_recv[s, g, c, t].astype(F32)
            tot_ref[s, g, t] = held.astype(BF16)
        for o in range(1, planes):
            @pl.when(sends_plane(s, o))
            def _():
                plane_copy(s, g, o).start()

    def turn_plane(s, g):
        for o in range(1, planes):
            @pl.when(takes_plane(s, o))
            def _():
                plane_copy(s, g, o).wait_recv()
        zero = tuple(jnp.zeros((part_rows, HEAD_DIM), F32) for _ in range(team))
        leap = [power(g * team + t, tok * row) for t in range(team)]

        def add(n, held):
            at = n if s == 0 else planes - 1 - n
            return tuple(
                leap[t] * held[t] + plane_recv[s, g, at, t].astype(F32) for t in range(team)
            )

        held = lax.fori_loop(0, z if s == 0 else planes - 1 - z, add, zero)
        for t in range(team):
            for c in range(row):
                far = power(g * team + t, tok * (c if s == 0 else row - 1 - c))
                full_ref[s, g, c, t] = (pre_ref[s, g, c, t] + far * held[t]).astype(BF16)
        for o in range(1, row):
            back_copy(s, g, o).start()
        back_recv[s, g, y] = full_ref[s, g, y]

    def end_scan(s, g):
        for o in range(1, row):
            back_copy(s, g, o).wait_recv()

    def crossing(s, h):
        g, t = divmod(h, team)
        return back_recv[s, g, :, t].reshape(HEAD_DIM, HEAD_DIM)

    leads = [powers(h, F32(tok) - positions) for h in range(heads)]
    load(1).wait()
    load(2).wait()
    for g in range(GROUPS):
        for h in range(g * team, (g + 1) * team):
            decayed = (k_ref[:, lanes(h)].astype(F32) * leads[h]).astype(BF16)
            put_state(0, h, dot(decayed, v_ref[:, lanes(h)], 0, 0))
        if g == 0:
            pl.semaphore_wait(barrier, row + planes + peers - 3)
        start_row(0, g)
    for n in range(3, 6):
        load(n).wait()
    gain = gain_ref[...].astype(F32).reshape(1, width)

    halves = tok // HALF
    blocks = [(r, c) for r in range(halves) for c in range(r + 1)]

    def rows_of(r):
        return slice(r * HALF, (r + 1) * HALF)

    def local_forward(h):
        at = lanes(h)
        offset = (
            lax.broadcasted_iota(jnp.int32, (HALF, HALF), 0)
            - lax.broadcasted_iota(jnp.int32, (HALF, HALF), 1)
        ).astype(F32)
        rate = rates[h][0:1, :]
        for d in range(halves):
            away = offset + F32(d * HALF)
            value = jnp.exp(jnp.maximum(away, 0.0) * rate)
            if d == 0:
                value = jnp.where(away >= 0, value, 0.0)
            decay_ref[h, d] = value
        for r in range(halves):
            total = None
            for c in range(r + 1):
                scores = dot(q_ref[rows_of(r), at], k_ref[rows_of(c), at], 1, 1)
                weights = (scores * decay_ref[h, r - c]).astype(BF16)
                w_ref[h, blocks.index((r, c))] = weights
                term = dot(weights, v_ref[rows_of(c), at], 1, 0)
                total = term if total is None else total + term
            att_ref[rows_of(r), at] = total
        after = powers(h, positions + 1.0)
        dq_ref[:, at] = (q_ref[:, at].astype(F32) * after).astype(BF16)
        near_ref[:, at] = powers(h, positions)
        far_ref[:, at] = powers(h, F32(tok - 1) - positions)
        gg_ref[:, at] = gain[:, at] * go_ref[:, at].astype(F32)

    third = (heads + 1) // 2

    def scan(s, local):
        for h in range(third):
            local(h)
        for g in range(GROUPS):
            turn_row(s, g)
        for h in range(third, (third + heads) // 2):
            local(h)
        for g in range(GROUPS):
            turn_plane(s, g)
        for h in range((third + heads) // 2, heads):
            local(h)

    scan(0, local_forward)

    squares = jnp.zeros((tok, HEAD_DIM), F32)
    crosses = jnp.zeros((tok, HEAD_DIM), F32)
    for h in range(heads):
        at = lanes(h)
        if h % team == 0:
            end_scan(0, h // team)
        att = att_ref[:, at] + near_ref[:, at] * dot(q_ref[:, at], crossing(0, h), 1, 0)
        att_ref[:, at] = att
        squares = squares + att * att
        crosses = crosses + gg_ref[:, at] * att
    part_ref[0:1, :] = jnp.sum(squares.T, axis=0, keepdims=True)
    part_ref[1:2, :] = jnp.sum(crosses.T, axis=0, keepdims=True)

    def peer_copy(o):
        return pltpu.make_async_remote_copy(
            src_ref=part_ref,
            dst_ref=peer_recv.at[me],
            send_sem=peer_send.at[o],
            recv_sem=peer_sem.at[o],
            device_id=(seq, lax.rem(me + o, peers)),
            device_id_type=MESH,
        )

    for o in range(1, peers):
        peer_copy(o).start()
    peer_recv[me] = part_ref[...]
    for o in range(1, peers):
        peer_copy(o).wait_recv()
    sums = peer_recv[0]
    for p in range(1, peers):
        sums = sums + peer_recv[p]
    features = F32(width * peers)
    inverse_row = lax.rsqrt(sums[0:1, :] / features + EPSILON)
    mean_row = inverse_row * sums[1:2, :] / features
    inverse = jnp.broadcast_to(inverse_row, (HEAD_DIM, tok)).T
    mean = jnp.broadcast_to(mean_row, (HEAD_DIM, tok)).T

    for h in range(heads):
        at = lanes(h)
        unit = att_ref[:, at] * inverse
        grad = (inverse * (gg_ref[:, at] - unit * mean)).astype(BF16)
        ga_ref[:, at] = grad
        put_state(1, h, dot(dq_ref[:, at], grad, 0, 0))
        if h % team == team - 1:
            start_row(1, h // team)
    for h in range(heads):
        at = lanes(h)
        norm_ref[:, at] = (att_ref[:, at] * inverse * gain[:, at]).astype(BF16)

    def local_backward(h):
        at = lanes(h)
        to_q = [None] * halves
        to_k = [None] * halves
        to_v = [None] * halves

        def add(old, new):
            return new if old is None else old + new

        for r, c in blocks:
            grad = ga_ref[rows_of(r), at]
            back = dot(grad, v_ref[rows_of(c), at], 1, 1)
            back = (back * decay_ref[h, r - c]).astype(BF16)
            to_q[r] = add(to_q[r], dot(back, k_ref[rows_of(c), at], 1, 0))
            to_k[c] = add(to_k[c], dot(back, q_ref[rows_of(r), at], 0, 0))
            to_v[c] = add(to_v[c], dot(w_ref[h, blocks.index((r, c))], grad, 0, 0))
        for r in range(halves):
            near = near_ref[rows_of(r), at]
            grad = ga_ref[rows_of(r), at]
            gq_ref[rows_of(r), at] = (
                to_q[r] + near * dot(grad, crossing(0, h), 1, 1)
            ).astype(BF16)
            acck_ref[rows_of(r), at] = to_k[r].astype(BF16)
            accv_ref[rows_of(r), at] = to_v[r].astype(BF16)

    scan(1, local_backward)
    for g in range(GROUPS):
        end_scan(1, g)
        for t in range(team):
            left_ref[g * team + t] = crossing(1, g * team + t)

    for s in range(2):
        for g in range(GROUPS):
            for o in range(1, row):
                row_copy(s, g, o).wait_send()
                back_copy(s, g, o).wait_send()
            for o in range(1, planes):
                @pl.when(sends_plane(s, o))
                def _():
                    plane_copy(s, g, o).wait_send()
    for o in range(1, peers):
        peer_copy(o).wait_send()


def finish(k_ref, v_ref, left_ref, norm_ref, gq_ref, acck_ref, accv_ref, far_ref,
           norm_out, gq_out, gk_out, gv_out, gk_ref, gv_ref, store_sem, part_sem):
    stores = [
        pltpu.make_async_copy(norm_ref, norm_out, store_sem.at[0]),
        pltpu.make_async_copy(gq_ref, gq_out, store_sem.at[1]),
    ]
    for store in stores:
        store.start()
    heads = left_ref.shape[0]
    for h in range(heads):
        at = slice(h * HEAD_DIM, (h + 1) * HEAD_DIM)
        far, left = far_ref[:, at], left_ref[h]
        gk_ref[:, at] = (
            acck_ref[:, at].astype(F32) + far * dot(v_ref[:, at], left, 1, 1)
        ).astype(BF16)
        gv_ref[:, at] = (
            accv_ref[:, at].astype(F32) + far * dot(k_ref[:, at], left, 1, 0)
        ).astype(BF16)
        if h % 2 == 1:
            both = slice((h - 1) * HEAD_DIM, (h + 1) * HEAD_DIM)
            for n, (src, dst) in enumerate(((gk_ref, gk_out), (gv_ref, gv_out))):
                stores.append(
                    pltpu.make_async_copy(
                        src.at[:, both], dst.at[:, both], part_sem.at[n, h // 2]
                    )
                )
                stores[-1].start()
    for store in stores:
        store.wait()


def body(row, planes, peers, queries, keys, values, decay_codes, gain, grad_out):
    tok, width = queries.shape
    heads = width // HEAD_DIM
    part_rows = HEAD_DIM // row
    halves = tok // HALF
    team = heads // GROUPS
    slices = (team, part_rows, HEAD_DIM)
    vmem = pl.BlockSpec(memory_space=pltpu.VMEM)
    far = pl.BlockSpec(memory_space=pltpu.HBM)
    out = jax.ShapeDtypeStruct((tok, width), BF16)
    wide = pltpu.VMEM((tok, width), F32)
    thin = pltpu.VMEM((tok, width), BF16)
    dma = pltpu.SemaphoreType.DMA
    normalized, grad_query, key_part, value_part, left, near_keys, near_values, far_powers = pl.pallas_call(
        functools.partial(kernel, row, planes, peers),
        out_shape=(thin,) * 4 + (pltpu.VMEM((heads, HEAD_DIM, HEAD_DIM), BF16), thin, thin, wide),
        in_specs=[far] * 6,
        out_specs=(vmem,) * 8,
        scratch_shapes=[pltpu.SMEM((heads,), jnp.int32), pltpu.VMEM((width,), BF16)] + [thin] * 2 + [
            pltpu.VMEM((heads, halves, HALF, HALF), F32),
            pltpu.VMEM((heads, halves * (halves + 1) // 2, HALF, HALF), BF16),
            wide, wide, thin, thin, wide,
            pltpu.VMEM((2, GROUPS, row) + slices, BF16),
            pltpu.VMEM((2, GROUPS, row) + slices, BF16),
            pltpu.VMEM((2, GROUPS, row) + slices, F32),
            pltpu.VMEM((2, GROUPS) + slices, BF16),
            pltpu.VMEM((2, GROUPS, planes) + slices, BF16),
            pltpu.VMEM((2, GROUPS, row) + slices, BF16),
            pltpu.VMEM((2, GROUPS, row) + slices, BF16),
            pltpu.VMEM((2, tok), F32),
            pltpu.VMEM((peers, 2, tok), F32),
            dma((6,)),
            dma((2 * GROUPS, row)),
            dma((2 * GROUPS, row)),
            dma((2 * GROUPS, planes)),
            dma((2 * GROUPS, planes)),
            dma((2 * GROUPS, row)),
            dma((2 * GROUPS, row)),
            dma((peers,)),
            dma((peers,)),
        ],
        compiler_params=pltpu.CompilerParams(
            collective_id=0, has_side_effects=True, vmem_limit_bytes=VMEM_A
        ),
        name="lightning",
    )(decay_codes, queries, keys, values, gain, grad_out)
    return pl.pallas_call(
        finish,
        out_shape=(out,) * 4,
        in_specs=[vmem] * 8,
        out_specs=(far,) * 4,
        scratch_shapes=[thin, thin, dma((2,)), dma((2, heads // 2))],
        compiler_params=pltpu.CompilerParams(vmem_limit_bytes=VMEM_B),
        name="finish",
    )(near_keys, near_values, left, normalized, grad_query, key_part, value_part, far_powers)


def solution(mesh):
    split = P("seq", "head")
    planes = mesh.shape["seq"] // ROW
    return jax.shard_map(
        functools.partial(body, ROW, planes, mesh.shape["head"]),
        mesh=mesh,
        in_specs=(split, split, split, P("head"), P("head"), split),
        out_specs=(split,) * 4,
        check_vma=False,
    )
```

```python
import functools

import jax
import jax.numpy as jnp
from jax import lax
from jax.experimental import pallas as pl
from jax.experimental.pallas import tpu as pltpu
from jax.sharding import PartitionSpec as P

HEAD_DIM = 128
EPSILON = 1e-06
ROW = 8
HALF = 256
GROUPS = 2
VMEM_A = 62600000
VMEM_B = 16777216
F32 = jnp.float32
BF16 = jnp.bfloat16
MESH = pl.DeviceIdType.MESH


def others(count):
    return sorted(range(1, count), key=lambda o: -min(o, count - o))


def dot(a, b, ca, cb):
    return lax.dot_general(a, b, (((ca,), (cb,)), ((), ())), preferred_element_type=F32)


def kernel(
    row, planes, peers,
    codes_hbm, q_hbm, k_hbm, v_hbm, gain_hbm, go_hbm,
    norm_ref, gq_ref, acck_ref, accv_ref, left_ref, k_ref, v_ref, far_ref,
    codes_ref, gain_ref, q_ref, go_ref,
    decay_ref, w_ref, att_ref, gg_ref, ga_ref, dq_ref, near_ref,
    state_ref, row_recv, pre_ref, tot_ref, plane_recv, full_ref, back_recv,
    part_ref, peer_recv, load_sem,
    row_send, row_sem, plane_send, plane_sem, back_send, back_sem, peer_send, peer_sem,
):
    tok, width = q_ref.shape
    heads = width // HEAD_DIM
    part_rows = HEAD_DIM // row
    team = heads // GROUPS
    seq = lax.axis_index("seq")
    me = lax.axis_index("head")
    z, y = seq // row, lax.rem(seq, row)

    def row_peer(o):
        return lax.rem(y + o, row)

    sources = (
        (codes_hbm, codes_ref), (k_hbm, k_ref), (v_hbm, v_ref),
        (q_hbm, q_ref), (gain_hbm, gain_ref), (go_hbm, go_ref),
    )

    def load(n):
        return pltpu.make_async_copy(*sources[n], load_sem.at[n])

    barrier = pltpu.get_barrier_semaphore()
    for o in others(row):
        pl.semaphore_signal(
            barrier, inc=1, device_id=(z * row + row_peer(o), me), device_id_type=MESH
        )
    for o in others(planes):
        pl.semaphore_signal(
            barrier, inc=1, device_id=(lax.rem(z + o, planes) * row + y, me), device_id_type=MESH
        )
    for o in others(peers):
        pl.semaphore_signal(
            barrier, inc=1, device_id=(seq, lax.rem(me + o, peers)), device_id_type=MESH
        )

    for n in range(6):
        load(n).start()

    def lanes(h):
        return slice(h * HEAD_DIM, (h + 1) * HEAD_DIM)

    load(0).wait()
    rates = []
    for h in range(heads):
        code = jnp.full((8, HALF), codes_ref[h], jnp.int32).astype(F32)
        rates.append(jnp.log1p(-jnp.exp2(-code)))

    positions = lax.broadcasted_iota(jnp.int32, (tok, HEAD_DIM), 0).astype(F32)

    def powers(h, exponent):
        return jnp.exp(exponent * rates[h][0:1, :HEAD_DIM])

    def power(h, n):
        return jnp.exp(F32(n) * rates[h][0:1, :HEAD_DIM])

    def row_copy(s, g, o):
        return pltpu.make_async_remote_copy(
            src_ref=state_ref.at[s, g, row_peer(o)],
            dst_ref=row_recv.at[s, g, y],
            send_sem=row_send.at[s * GROUPS + g, o],
            recv_sem=row_sem.at[s * GROUPS + g, o],
            device_id=(z * row + row_peer(o), me),
            device_id_type=MESH,
        )

    def plane_copy(s, g, o):
        to = z + o if s == 0 else z - o
        return pltpu.make_async_remote_copy(
            src_ref=tot_ref.at[s, g],
            dst_ref=plane_recv.at[s, g, z],
            send_sem=plane_send.at[s * GROUPS + g, o],
            recv_sem=plane_sem.at[s * GROUPS + g, o],
            device_id=(lax.rem(to + planes, planes) * row + y, me),
            device_id_type=MESH,
        )

    def back_copy(s, g, o):
        return pltpu.make_async_remote_copy(
            src_ref=full_ref.at[s, g, row_peer(o)],
            dst_ref=back_recv.at[s, g, y],
            send_sem=back_send.at[s * GROUPS + g, o],
            recv_sem=back_sem.at[s * GROUPS + g, o],
            device_id=(z * row + row_peer(o), me),
            device_id_type=MESH,
        )

    def sends_plane(s, o):
        return z + o < planes if s == 0 else z - o >= 0

    def takes_plane(s, o):
        return z - o >= 0 if s == 0 else z + o < planes

    def put_state(s, h, value):
        g, t = divmod(h, team)
        state_ref[s, g, :, t] = value.astype(BF16).reshape(row, part_rows, HEAD_DIM)

    def start_row(s, g):
        for o in others(row):
            row_copy(s, g, o).start()
        row_recv[s, g, y] = state_ref[s, g, y]

    def turn_row(s, g):
        for o in others(row):
            row_copy(s, g, o).wait_recv()
        for t in range(team):
            step = power(g * team + t, tok)
            held = jnp.zeros((part_rows, HEAD_DIM), F32)
            for c in range(row) if s == 0 else reversed(range(row)):
                pre_ref[s, g, c, t] = held
                held = step * held + row_recv[s, g, c, t].astype(F32)
            tot_ref[s, g, t] = held.astype(BF16)
        for o in others(planes):
            @pl.when(sends_plane(s, o))
            def _():
                plane_copy(s, g, o).start()

    def turn_plane(s, g):
        for o in others(planes):
            @pl.when(takes_plane(s, o))
            def _():
                plane_copy(s, g, o).wait_recv()
        zero = tuple(jnp.zeros((part_rows, HEAD_DIM), F32) for _ in range(team))
        leap = [power(g * team + t, tok * row) for t in range(team)]

        def add(n, held):
            at = n if s == 0 else planes - 1 - n
            return tuple(
                leap[t] * held[t] + plane_recv[s, g, at, t].astype(F32) for t in range(team)
            )

        held = lax.fori_loop(0, z if s == 0 else planes - 1 - z, add, zero)
        for t in range(team):
            for c in range(row):
                far = power(g * team + t, tok * (c if s == 0 else row - 1 - c))
                full_ref[s, g, c, t] = (pre_ref[s, g, c, t] + far * held[t]).astype(BF16)
        for o in others(row):
            back_copy(s, g, o).start()
        back_recv[s, g, y] = full_ref[s, g, y]

    def end_scan(s, g):
        for o in others(row):
            back_copy(s, g, o).wait_recv()

    def crossing(s, h):
        g, t = divmod(h, team)
        return back_recv[s, g, :, t].reshape(HEAD_DIM, HEAD_DIM)

    leads = [powers(h, F32(tok) - positions) for h in range(heads)]
    load(1).wait()
    load(2).wait()
    for g in range(GROUPS):
        for h in range(g * team, (g + 1) * team):
            decayed = (k_ref[:, lanes(h)].astype(F32) * leads[h]).astype(BF16)
            put_state(0, h, dot(decayed, v_ref[:, lanes(h)], 0, 0))
        if g == 0:
            pl.semaphore_wait(barrier, row + planes + peers - 3)
        start_row(0, g)
    for n in range(3, 6):
        load(n).wait()
    gain = gain_ref[...].astype(F32).reshape(1, width)

    halves = tok // HALF
    blocks = [(r, c) for r in range(halves) for c in range(r + 1)]

    def rows_of(r):
        return slice(r * HALF, (r + 1) * HALF)

    def local_forward(h):
        at = lanes(h)
        offset = (
            lax.broadcasted_iota(jnp.int32, (HALF, HALF), 0)
            - lax.broadcasted_iota(jnp.int32, (HALF, HALF), 1)
        ).astype(F32)
        rate = rates[h][0:1, :]
        for d in range(halves):
            away = offset + F32(d * HALF)
            value = jnp.exp(jnp.maximum(away, 0.0) * rate)
            if d == 0:
                value = jnp.where(away >= 0, value, 0.0)
            decay_ref[h, d] = value
        for r in range(halves):
            total = None
            for c in range(r + 1):
                scores = dot(q_ref[rows_of(r), at], k_ref[rows_of(c), at], 1, 1)
                weights = (scores * decay_ref[h, r - c]).astype(BF16)
                w_ref[h, blocks.index((r, c))] = weights
                term = dot(weights, v_ref[rows_of(c), at], 1, 0)
                total = term if total is None else total + term
            att_ref[rows_of(r), at] = total
        after = powers(h, positions + 1.0)
        dq_ref[h] = (q_ref[:, at].astype(F32) * after).astype(BF16).T
        near_ref[:, at] = powers(h, positions)
        far_ref[:, at] = powers(h, F32(tok - 1) - positions)
        gg_ref[:, at] = gain[:, at] * go_ref[:, at].astype(F32)

    third = (heads + 1) // 2

    def scan(s, local):
        for h in range(third):
            local(h)
        for g in range(GROUPS):
            turn_row(s, g)
        for h in range(third, (third + heads) // 2):
            local(h)
        for g in range(GROUPS):
            turn_plane(s, g)
        for h in range((third + heads) // 2, heads):
            local(h)

    scan(0, local_forward)

    squares = jnp.zeros((tok, HEAD_DIM), F32)
    crosses = jnp.zeros((tok, HEAD_DIM), F32)
    for h in range(heads):
        at = lanes(h)
        if h % team == 0:
            end_scan(0, h // team)
        att = att_ref[:, at] + near_ref[:, at] * dot(q_ref[:, at], crossing(0, h), 1, 0)
        att_ref[:, at] = att
        squares = squares + att * att
        crosses = crosses + gg_ref[:, at] * att
    part_ref[0:1, :] = jnp.sum(squares.T, axis=0, keepdims=True)
    part_ref[1:2, :] = jnp.sum(crosses.T, axis=0, keepdims=True)

    def peer_copy(o):
        return pltpu.make_async_remote_copy(
            src_ref=part_ref,
            dst_ref=peer_recv.at[me],
            send_sem=peer_send.at[o],
            recv_sem=peer_sem.at[o],
            device_id=(seq, lax.rem(me + o, peers)),
            device_id_type=MESH,
        )

    for o in others(peers):
        peer_copy(o).start()
    peer_recv[me] = part_ref[...]
    for o in others(peers):
        peer_copy(o).wait_recv()
    sums = peer_recv[0]
    for p in range(1, peers):
        sums = sums + peer_recv[p]
    features = F32(width * peers)
    inverse_row = lax.rsqrt(sums[0:1, :] / features + EPSILON)
    mean_row = inverse_row * sums[1:2, :] / features
    inverse = jnp.broadcast_to(inverse_row, (HEAD_DIM, tok)).T
    mean = jnp.broadcast_to(mean_row, (HEAD_DIM, tok)).T

    for h in range(heads):
        at = lanes(h)
        unit = att_ref[:, at] * inverse
        grad = (inverse * (gg_ref[:, at] - unit * mean)).astype(BF16)
        ga_ref[:, at] = grad
        put_state(1, h, dot(dq_ref[h], grad, 1, 0))
        if h % team == team - 1:
            start_row(1, h // team)
    for h in range(heads):
        at = lanes(h)
        norm_ref[:, at] = (att_ref[:, at] * inverse * gain[:, at]).astype(BF16)

    def local_backward(h):
        at = lanes(h)
        to_q = [None] * halves
        to_k = [None] * halves
        to_v = [None] * halves

        def add(old, new):
            return new if old is None else old + new

        for r, c in blocks:
            grad = ga_ref[rows_of(r), at]
            back = dot(grad, v_ref[rows_of(c), at], 1, 1)
            back = (back * decay_ref[h, r - c]).astype(BF16)
            to_q[r] = add(to_q[r], dot(back, k_ref[rows_of(c), at], 1, 0))
            to_k[c] = add(to_k[c], dot(back, q_ref[rows_of(r), at], 0, 0))
            to_v[c] = add(to_v[c], dot(w_ref[h, blocks.index((r, c))], grad, 0, 0))
        for r in range(halves):
            near = near_ref[rows_of(r), at]
            grad = ga_ref[rows_of(r), at]
            gq_ref[rows_of(r), at] = (
                to_q[r] + near * dot(grad, crossing(0, h), 1, 1)
            ).astype(BF16)
            acck_ref[rows_of(r), at] = to_k[r].astype(BF16)
            accv_ref[rows_of(r), at] = to_v[r].astype(BF16)

    scan(1, local_backward)
    for g in range(GROUPS):
        end_scan(1, g)
        for t in range(team):
            left_ref[g * team + t] = crossing(1, g * team + t)

    for s in range(2):
        for g in range(GROUPS):
            for o in others(row):
                row_copy(s, g, o).wait_send()
                back_copy(s, g, o).wait_send()
            for o in others(planes):
                @pl.when(sends_plane(s, o))
                def _():
                    plane_copy(s, g, o).wait_send()
    for o in others(peers):
        peer_copy(o).wait_send()


def finish(k_ref, v_ref, left_ref, norm_ref, gq_ref, acck_ref, accv_ref, far_ref,
           norm_out, gq_out, gk_out, gv_out, gk_ref, gv_ref, store_sem, part_sem):
    stores = [
        pltpu.make_async_copy(norm_ref, norm_out, store_sem.at[0]),
        pltpu.make_async_copy(gq_ref, gq_out, store_sem.at[1]),
    ]
    for store in stores:
        store.start()
    heads = left_ref.shape[0]
    for h in range(heads):
        at = slice(h * HEAD_DIM, (h + 1) * HEAD_DIM)
        far, left = far_ref[:, at], left_ref[h]
        gk_ref[:, at] = (
            acck_ref[:, at].astype(F32) + far * dot(v_ref[:, at], left, 1, 1)
        ).astype(BF16)
        gv_ref[:, at] = (
            accv_ref[:, at].astype(F32) + far * dot(k_ref[:, at], left, 1, 0)
        ).astype(BF16)
        if h % 2 == 1:
            both = slice((h - 1) * HEAD_DIM, (h + 1) * HEAD_DIM)
            for n, (src, dst) in enumerate(((gk_ref, gk_out), (gv_ref, gv_out))):
                stores.append(
                    pltpu.make_async_copy(
                        src.at[:, both], dst.at[:, both], part_sem.at[n, h // 2]
                    )
                )
                stores[-1].start()
    for store in stores:
        store.wait()


def body(row, planes, peers, queries, keys, values, decay_codes, gain, grad_out):
    tok, width = queries.shape
    heads = width // HEAD_DIM
    part_rows = HEAD_DIM // row
    halves = tok // HALF
    team = heads // GROUPS
    slices = (team, part_rows, HEAD_DIM)
    vmem = pl.BlockSpec(memory_space=pltpu.VMEM)
    far = pl.BlockSpec(memory_space=pltpu.HBM)
    out = jax.ShapeDtypeStruct((tok, width), BF16)
    wide = pltpu.VMEM((tok, width), F32)
    thin = pltpu.VMEM((tok, width), BF16)
    dma = pltpu.SemaphoreType.DMA
    normalized, grad_query, key_part, value_part, left, near_keys, near_values, far_powers = pl.pallas_call(
        functools.partial(kernel, row, planes, peers),
        out_shape=(thin,) * 4 + (pltpu.VMEM((heads, HEAD_DIM, HEAD_DIM), BF16), thin, thin, wide),
        in_specs=[far] * 6,
        out_specs=(vmem,) * 8,
        scratch_shapes=[pltpu.SMEM((heads,), jnp.int32), pltpu.VMEM((width,), BF16)] + [thin] * 2 + [
            pltpu.VMEM((heads, halves, HALF, HALF), F32),
            pltpu.VMEM((heads, halves * (halves + 1) // 2, HALF, HALF), BF16),
            wide, wide, thin, pltpu.VMEM((heads, HEAD_DIM, tok), BF16), wide,
            pltpu.VMEM((2, GROUPS, row) + slices, BF16),
            pltpu.VMEM((2, GROUPS, row) + slices, BF16),
            pltpu.VMEM((2, GROUPS, row) + slices, F32),
            pltpu.VMEM((2, GROUPS) + slices, BF16),
            pltpu.VMEM((2, GROUPS, planes) + slices, BF16),
            pltpu.VMEM((2, GROUPS, row) + slices, BF16),
            pltpu.VMEM((2, GROUPS, row) + slices, BF16),
            pltpu.VMEM((2, tok), F32),
            pltpu.VMEM((peers, 2, tok), F32),
            dma((6,)),
            dma((2 * GROUPS, row)),
            dma((2 * GROUPS, row)),
            dma((2 * GROUPS, planes)),
            dma((2 * GROUPS, planes)),
            dma((2 * GROUPS, row)),
            dma((2 * GROUPS, row)),
            dma((peers,)),
            dma((peers,)),
        ],
        compiler_params=pltpu.CompilerParams(
            collective_id=0, has_side_effects=True, vmem_limit_bytes=VMEM_A
        ),
        name="lightning",
    )(decay_codes, queries, keys, values, gain, grad_out)
    return pl.pallas_call(
        finish,
        out_shape=(out,) * 4,
        in_specs=[vmem] * 8,
        out_specs=(far,) * 4,
        scratch_shapes=[thin, thin, dma((2,)), dma((2, heads // 2))],
        compiler_params=pltpu.CompilerParams(vmem_limit_bytes=VMEM_B),
        name="finish",
    )(near_keys, near_values, left, normalized, grad_query, key_part, value_part, far_powers)


def solution(mesh):
    split = P("seq", "head")
    planes = mesh.shape["seq"] // ROW
    return jax.shard_map(
        functools.partial(body, ROW, planes, mesh.shape["head"]),
        mesh=mesh,
        in_specs=(split, split, split, P("head"), P("head"), split),
        out_specs=(split,) * 4,
        check_vma=False,
    )
```

```python
import functools

import jax
import jax.numpy as jnp
from jax import lax
from jax.experimental import pallas as pl
from jax.experimental.pallas import tpu as pltpu
from jax.sharding import PartitionSpec as P

HEAD_DIM = 128
EPSILON = 1e-06
ROW = 8
HALF = 256
GROUPS = 2
VMEM_A = 62600000
VMEM_B = 16777216
F32 = jnp.float32
BF16 = jnp.bfloat16
MESH = pl.DeviceIdType.MESH


def others(count):
    return sorted(range(1, count), key=lambda o: -min(o, count - o))


def dot(a, b, ca, cb):
    return lax.dot_general(a, b, (((ca,), (cb,)), ((), ())), preferred_element_type=F32)


def kernel(
    row, planes, peers,
    codes_hbm, q_hbm, k_hbm, v_hbm, gain_hbm, go_hbm,
    norm_ref, gq_ref, acck_ref, accv_ref, left_ref, k_ref, v_ref, far_ref,
    codes_ref, gain_ref, q_ref, go_ref,
    decay_ref, w_ref, att_ref, gg_ref, ga_ref, dq_ref, near_ref,
    state_ref, row_recv, pre_ref, tot_ref, plane_recv, full_ref, back_recv,
    part_ref, peer_recv, load_sem,
    row_send, row_sem, plane_send, plane_sem, back_send, back_sem, peer_send, peer_sem,
):
    tok, width = q_ref.shape
    heads = width // HEAD_DIM
    part_rows = HEAD_DIM // row
    team = heads // GROUPS
    seq = lax.axis_index("seq")
    me = lax.axis_index("head")
    z, y = seq // row, lax.rem(seq, row)

    def row_peer(o):
        return lax.rem(y + o, row)

    sources = (
        (codes_hbm, codes_ref), (k_hbm, k_ref), (v_hbm, v_ref),
        (q_hbm, q_ref), (gain_hbm, gain_ref), (go_hbm, go_ref),
    )

    def load(n):
        return pltpu.make_async_copy(*sources[n], load_sem.at[n])

    barrier = pltpu.get_barrier_semaphore()
    for o in others(row):
        pl.semaphore_signal(
            barrier, inc=1, device_id=(z * row + row_peer(o), me), device_id_type=MESH
        )
    for o in others(planes):
        pl.semaphore_signal(
            barrier, inc=1, device_id=(lax.rem(z + o, planes) * row + y, me), device_id_type=MESH
        )
    for o in others(peers):
        pl.semaphore_signal(
            barrier, inc=1, device_id=(seq, lax.rem(me + o, peers)), device_id_type=MESH
        )

    for n in range(6):
        load(n).start()

    def lanes(h):
        return slice(h * HEAD_DIM, (h + 1) * HEAD_DIM)

    load(0).wait()
    rates = []
    for h in range(heads):
        code = jnp.full((8, HALF), codes_ref[h], jnp.int32).astype(F32)
        rates.append(jnp.log1p(-jnp.exp2(-code)))

    positions = lax.broadcasted_iota(jnp.int32, (tok, HEAD_DIM), 0).astype(F32)

    def powers(h, exponent):
        return jnp.exp(exponent * rates[h][0:1, :HEAD_DIM])

    def power(h, n):
        return jnp.exp(F32(n) * rates[h][0:1, :HEAD_DIM])

    def row_copy(s, g, o):
        return pltpu.make_async_remote_copy(
            src_ref=state_ref.at[s, g, row_peer(o)],
            dst_ref=row_recv.at[s, g, y],
            send_sem=row_send.at[s * GROUPS + g, o],
            recv_sem=row_sem.at[s * GROUPS + g, o],
            device_id=(z * row + row_peer(o), me),
            device_id_type=MESH,
        )

    def plane_copy(s, g, o):
        to = z + o if s == 0 else z - o
        return pltpu.make_async_remote_copy(
            src_ref=tot_ref.at[s, g],
            dst_ref=plane_recv.at[s, g, z],
            send_sem=plane_send.at[s * GROUPS + g, o],
            recv_sem=plane_sem.at[s * GROUPS + g, o],
            device_id=(lax.rem(to + planes, planes) * row + y, me),
            device_id_type=MESH,
        )

    def back_copy(s, g, o):
        return pltpu.make_async_remote_copy(
            src_ref=full_ref.at[s, g, row_peer(o)],
            dst_ref=back_recv.at[s, g, y],
            send_sem=back_send.at[s * GROUPS + g, o],
            recv_sem=back_sem.at[s * GROUPS + g, o],
            device_id=(z * row + row_peer(o), me),
            device_id_type=MESH,
        )

    def sends_plane(s, o):
        return z + o < planes if s == 0 else z - o >= 0

    def takes_plane(s, o):
        return z - o >= 0 if s == 0 else z + o < planes

    def put_state(s, h, value):
        g, t = divmod(h, team)
        state_ref[s, g, :, t] = value.astype(BF16).reshape(row, part_rows, HEAD_DIM)

    def start_row(s, g):
        for o in others(row):
            row_copy(s, g, o).start()
        row_recv[s, g, y] = state_ref[s, g, y]

    def turn_row(s, g):
        steps = [power(g * team + t, tok) for t in range(team)]
        for o in others(row):
            row_copy(s, g, o).wait_recv()
        for t in range(team):
            held = jnp.zeros((part_rows, HEAD_DIM), F32)
            for c in range(row) if s == 0 else reversed(range(row)):
                pre_ref[s, g, c, t] = held
                held = steps[t] * held + row_recv[s, g, c, t].astype(F32)
            tot_ref[s, g, t] = held.astype(BF16)
        for o in others(planes):
            @pl.when(sends_plane(s, o))
            def _():
                plane_copy(s, g, o).start()

    def turn_plane(s, g):
        leap = [power(g * team + t, tok * row) for t in range(team)]
        fars = [
            [power(g * team + t, tok * (c if s == 0 else row - 1 - c)) for c in range(row)]
            for t in range(team)
        ]
        for o in others(planes):
            @pl.when(takes_plane(s, o))
            def _():
                plane_copy(s, g, o).wait_recv()
        zero = tuple(jnp.zeros((part_rows, HEAD_DIM), F32) for _ in range(team))

        def add(n, held):
            at = n if s == 0 else planes - 1 - n
            return tuple(
                leap[t] * held[t] + plane_recv[s, g, at, t].astype(F32) for t in range(team)
            )

        held = lax.fori_loop(0, z if s == 0 else planes - 1 - z, add, zero)
        for t in range(team):
            for c in range(row):
                full_ref[s, g, c, t] = (pre_ref[s, g, c, t] + fars[t][c] * held[t]).astype(BF16)
        for o in others(row):
            back_copy(s, g, o).start()
        back_recv[s, g, y] = full_ref[s, g, y]

    def end_scan(s, g):
        for o in others(row):
            back_copy(s, g, o).wait_recv()

    def crossing(s, h):
        g, t = divmod(h, team)
        return back_recv[s, g, :, t].reshape(HEAD_DIM, HEAD_DIM)

    leads = [powers(h, F32(tok) - positions) for h in range(heads)]
    load(1).wait()
    load(2).wait()
    for g in range(GROUPS):
        for h in range(g * team, (g + 1) * team):
            decayed = (k_ref[:, lanes(h)].astype(F32) * leads[h]).astype(BF16)
            put_state(0, h, dot(decayed, v_ref[:, lanes(h)], 0, 0))
        if g == 0:
            pl.semaphore_wait(barrier, row + planes + peers - 3)
        start_row(0, g)
    for n in range(3, 6):
        load(n).wait()
    gain = gain_ref[...].astype(F32).reshape(1, width)

    halves = tok // HALF
    blocks = [(r, c) for r in range(halves) for c in range(r + 1)]

    def rows_of(r):
        return slice(r * HALF, (r + 1) * HALF)

    def local_forward(h):
        at = lanes(h)
        offset = (
            lax.broadcasted_iota(jnp.int32, (HALF, HALF), 0)
            - lax.broadcasted_iota(jnp.int32, (HALF, HALF), 1)
        ).astype(F32)
        rate = rates[h][0:1, :]
        for d in range(halves):
            away = offset + F32(d * HALF)
            value = jnp.exp(jnp.maximum(away, 0.0) * rate)
            if d == 0:
                value = jnp.where(away >= 0, value, 0.0)
            decay_ref[h, d] = value
        for r in range(halves):
            total = None
            for c in range(r + 1):
                scores = dot(q_ref[rows_of(r), at], k_ref[rows_of(c), at], 1, 1)
                weights = (scores * decay_ref[h, r - c]).astype(BF16)
                w_ref[h, blocks.index((r, c))] = weights
                term = dot(weights, v_ref[rows_of(c), at], 1, 0)
                total = term if total is None else total + term
            att_ref[rows_of(r), at] = total
        after = powers(h, positions + 1.0)
        dq_ref[h] = (q_ref[:, at].astype(F32) * after).astype(BF16).T
        near_ref[:, at] = powers(h, positions)
        far_ref[:, at] = powers(h, F32(tok - 1) - positions)
        gg_ref[:, at] = gain[:, at] * go_ref[:, at].astype(F32)

    third = (heads + 1) // 2

    def scan(s, local):
        for h in range(third):
            local(h)
        for g in range(GROUPS):
            turn_row(s, g)
        for h in range(third, (third + heads) // 2):
            local(h)
        for g in range(GROUPS):
            turn_plane(s, g)
        for h in range((third + heads) // 2, heads):
            local(h)

    scan(0, local_forward)

    squares = jnp.zeros((tok, HEAD_DIM), F32)
    crosses = jnp.zeros((tok, HEAD_DIM), F32)
    for h in range(heads):
        at = lanes(h)
        if h % team == 0:
            end_scan(0, h // team)
        att = att_ref[:, at] + near_ref[:, at] * dot(q_ref[:, at], crossing(0, h), 1, 0)
        att_ref[:, at] = att
        squares = squares + att * att
        crosses = crosses + gg_ref[:, at] * att
    part_ref[0:1, :] = jnp.sum(squares.T, axis=0, keepdims=True)
    part_ref[1:2, :] = jnp.sum(crosses.T, axis=0, keepdims=True)

    def peer_copy(o):
        return pltpu.make_async_remote_copy(
            src_ref=part_ref,
            dst_ref=peer_recv.at[me],
            send_sem=peer_send.at[o],
            recv_sem=peer_sem.at[o],
            device_id=(seq, lax.rem(me + o, peers)),
            device_id_type=MESH,
        )

    for o in others(peers):
        peer_copy(o).start()
    peer_recv[me] = part_ref[...]
    for o in others(peers):
        peer_copy(o).wait_recv()
    sums = peer_recv[0]
    for p in range(1, peers):
        sums = sums + peer_recv[p]
    features = F32(width * peers)
    inverse_row = lax.rsqrt(sums[0:1, :] / features + EPSILON)
    mean_row = inverse_row * sums[1:2, :] / features
    inverse = jnp.broadcast_to(inverse_row, (HEAD_DIM, tok)).T
    mean = jnp.broadcast_to(mean_row, (HEAD_DIM, tok)).T

    for h in range(heads):
        at = lanes(h)
        unit = att_ref[:, at] * inverse
        grad = (inverse * (gg_ref[:, at] - unit * mean)).astype(BF16)
        ga_ref[:, at] = grad
        put_state(1, h, dot(dq_ref[h], grad, 1, 0))
        if h % team == team - 1:
            start_row(1, h // team)
    for h in range(heads):
        at = lanes(h)
        norm_ref[:, at] = (att_ref[:, at] * inverse * gain[:, at]).astype(BF16)

    def local_backward(h):
        at = lanes(h)
        to_q = [None] * halves
        to_k = [None] * halves
        to_v = [None] * halves

        def add(old, new):
            return new if old is None else old + new

        for r, c in blocks:
            grad = ga_ref[rows_of(r), at]
            back = dot(grad, v_ref[rows_of(c), at], 1, 1)
            back = (back * decay_ref[h, r - c]).astype(BF16)
            to_q[r] = add(to_q[r], dot(back, k_ref[rows_of(c), at], 1, 0))
            to_k[c] = add(to_k[c], dot(back, q_ref[rows_of(r), at], 0, 0))
            to_v[c] = add(to_v[c], dot(w_ref[h, blocks.index((r, c))], grad, 0, 0))
        for r in range(halves):
            near = near_ref[rows_of(r), at]
            grad = ga_ref[rows_of(r), at]
            gq_ref[rows_of(r), at] = (
                to_q[r] + near * dot(grad, crossing(0, h), 1, 1)
            ).astype(BF16)
            acck_ref[rows_of(r), at] = to_k[r].astype(BF16)
            accv_ref[rows_of(r), at] = to_v[r].astype(BF16)

    scan(1, local_backward)
    for g in range(GROUPS):
        end_scan(1, g)
        for t in range(team):
            left_ref[g * team + t] = crossing(1, g * team + t)

    for s in range(2):
        for g in range(GROUPS):
            for o in others(row):
                row_copy(s, g, o).wait_send()
                back_copy(s, g, o).wait_send()
            for o in others(planes):
                @pl.when(sends_plane(s, o))
                def _():
                    plane_copy(s, g, o).wait_send()
    for o in others(peers):
        peer_copy(o).wait_send()


def finish(k_ref, v_ref, left_ref, norm_ref, gq_ref, acck_ref, accv_ref, far_ref,
           norm_out, gq_out, gk_out, gv_out, gk_ref, gv_ref, store_sem, part_sem):
    stores = [
        pltpu.make_async_copy(norm_ref, norm_out, store_sem.at[0]),
        pltpu.make_async_copy(gq_ref, gq_out, store_sem.at[1]),
    ]
    for store in stores:
        store.start()
    heads = left_ref.shape[0]
    for h in range(heads):
        at = slice(h * HEAD_DIM, (h + 1) * HEAD_DIM)
        far, left = far_ref[:, at], left_ref[h]
        gk_ref[:, at] = (
            acck_ref[:, at].astype(F32) + far * dot(v_ref[:, at], left, 1, 1)
        ).astype(BF16)
        gv_ref[:, at] = (
            accv_ref[:, at].astype(F32) + far * dot(k_ref[:, at], left, 1, 0)
        ).astype(BF16)
        if h % 2 == 1:
            both = slice((h - 1) * HEAD_DIM, (h + 1) * HEAD_DIM)
            for n, (src, dst) in enumerate(((gk_ref, gk_out), (gv_ref, gv_out))):
                stores.append(
                    pltpu.make_async_copy(
                        src.at[:, both], dst.at[:, both], part_sem.at[n, h // 2]
                    )
                )
                stores[-1].start()
    for store in stores:
        store.wait()


def body(row, planes, peers, queries, keys, values, decay_codes, gain, grad_out):
    tok, width = queries.shape
    heads = width // HEAD_DIM
    part_rows = HEAD_DIM // row
    halves = tok // HALF
    team = heads // GROUPS
    slices = (team, part_rows, HEAD_DIM)
    vmem = pl.BlockSpec(memory_space=pltpu.VMEM)
    far = pl.BlockSpec(memory_space=pltpu.HBM)
    out = jax.ShapeDtypeStruct((tok, width), BF16)
    wide = pltpu.VMEM((tok, width), F32)
    thin = pltpu.VMEM((tok, width), BF16)
    dma = pltpu.SemaphoreType.DMA
    normalized, grad_query, key_part, value_part, left, near_keys, near_values, far_powers = pl.pallas_call(
        functools.partial(kernel, row, planes, peers),
        out_shape=(thin,) * 4 + (pltpu.VMEM((heads, HEAD_DIM, HEAD_DIM), BF16), thin, thin, wide),
        in_specs=[far] * 6,
        out_specs=(vmem,) * 8,
        scratch_shapes=[pltpu.SMEM((heads,), jnp.int32), pltpu.VMEM((width,), BF16)] + [thin] * 2 + [
            pltpu.VMEM((heads, halves, HALF, HALF), F32),
            pltpu.VMEM((heads, halves * (halves + 1) // 2, HALF, HALF), BF16),
            wide, wide, thin, pltpu.VMEM((heads, HEAD_DIM, tok), BF16), wide,
            pltpu.VMEM((2, GROUPS, row) + slices, BF16),
            pltpu.VMEM((2, GROUPS, row) + slices, BF16),
            pltpu.VMEM((2, GROUPS, row) + slices, F32),
            pltpu.VMEM((2, GROUPS) + slices, BF16),
            pltpu.VMEM((2, GROUPS, planes) + slices, BF16),
            pltpu.VMEM((2, GROUPS, row) + slices, BF16),
            pltpu.VMEM((2, GROUPS, row) + slices, BF16),
            pltpu.VMEM((2, tok), F32),
            pltpu.VMEM((peers, 2, tok), F32),
            dma((6,)),
            dma((2 * GROUPS, row)),
            dma((2 * GROUPS, row)),
            dma((2 * GROUPS, planes)),
            dma((2 * GROUPS, planes)),
            dma((2 * GROUPS, row)),
            dma((2 * GROUPS, row)),
            dma((peers,)),
            dma((peers,)),
        ],
        compiler_params=pltpu.CompilerParams(
            collective_id=0, has_side_effects=True, vmem_limit_bytes=VMEM_A
        ),
        name="lightning",
    )(decay_codes, queries, keys, values, gain, grad_out)
    return pl.pallas_call(
        finish,
        out_shape=(out,) * 4,
        in_specs=[vmem] * 8,
        out_specs=(far,) * 4,
        scratch_shapes=[thin, thin, dma((2,)), dma((2, heads // 2))],
        compiler_params=pltpu.CompilerParams(vmem_limit_bytes=VMEM_B),
        name="finish",
    )(near_keys, near_values, left, normalized, grad_query, key_part, value_part, far_powers)


def solution(mesh):
    split = P("seq", "head")
    planes = mesh.shape["seq"] // ROW
    return jax.shard_map(
        functools.partial(body, ROW, planes, mesh.shape["head"]),
        mesh=mesh,
        in_specs=(split, split, split, P("head"), P("head"), split),
        out_specs=(split,) * 4,
        check_vma=False,
    )
```
